32 devices in a mesh: harm: 16 (over z, x, core), bus: 2 (over y).
Axes of the slice: x: 2, y: 2, z: 4, core: 2. Of those that a mesh axis runs over, the one named last changes fastest.
Arguments:
- conv_volt: bfloat16 [2, 64, 128, 128], P(None, None, ('bus', 'harm')), may hold values from -0.75 to 0.75
- conv_power: float32 [128, 128], P(('bus', 'harm')), may hold values from 0.2 to 2
- conv_type: int32 [128], P(('bus', 'harm')), may hold values from 0 to 7
- type_steep: float32 [8], replicated, may hold values from 0.5 to 4
- conv_bus: int32 [128], P(('bus', 'harm')), may hold values from 0 to 511, as said below
- admittance: float32 [2, 4, 64, 512], P(None, None, 'harm', 'bus'), may hold values from -0.5 to 1
- link_offset: int32 [3, 512], P(None, 'bus'), may hold values from -8 to 8, as said below
Outputs:
- bus_volt: bfloat16 [2, 64, 512, 128], P(None, 'harm', 'bus')
- conv_next: bfloat16 [2, 64, 128, 128], P(None, None, ('bus', 'harm'))
The draws below stay inside these ranges and needn't reach their ends.
Inputs may be any that keep to these rules, and one draw needn't show every extreme that they name: `conv_bus`: converter c is attached to one of the buses from (c // 4) * 16 to (c // 4 + 1) * 16 - 1; a bus may carry several converters. `link_offset`: the first line of every bus spans exactly 8 buses, up or down; the others span 1 to 8 buses; no offset is zero.
All inputs are finite; a program needn't handle non-finite values.
Results may differ from the reference program's by a relative error of at most 0.0057.
Values may be sent and summed in bfloat16 or wider, within the bound.
A program may use at most 64 MiB of HBM per device.

```python
import math
import jax
import jax.numpy as jnp
from jax import lax

H = 64
NT = 1024
S = 128
CONV_DEV = 4
BUS_SUB = 16
TYPES = 8
LINKS = 3
REACH = 8
ITERS = 3
CONVS = 128
BUSES = 512


def draw_conv_bus(key, part):
    keys = jax.random.split(jax.random.fold_in(key, 11), 3)
    first_pick = jax.random.randint(keys[0], (CONVS,), 0, BUS_SUB)
    second_pick = jax.random.randint(keys[1], (CONVS,), 0, BUS_SUB)
    rotation = jax.random.randint(keys[2], (CONVS // CONV_DEV,), 0, BUS_SUB)
    group_num = jnp.arange(CONVS, dtype=jnp.int32) // CONV_DEV
    local_bus = (jnp.minimum(first_pick, second_pick) + rotation[group_num]) % BUS_SUB
    return (group_num * BUS_SUB + local_bus).astype(jnp.int32)


def draw_link_offset(key, part):
    keys = jax.random.split(jax.random.fold_in(key, 23), 2)
    distance = jax.random.randint(keys[0], (LINKS, BUSES), 1, REACH + 1)
    distance = jnp.where(jnp.arange(LINKS, dtype=jnp.int32)[:, None] == 0, REACH, distance)
    direction = jax.random.randint(keys[1], (LINKS, BUSES), 0, 2) * 2 - 1
    return (distance * direction).astype(jnp.int32)


def draw_admittance(key, part):
    keys = jax.random.split(jax.random.fold_in(key, 37), 3)
    inverse_real = jax.random.uniform(keys[0], (H, BUSES), jnp.float32, 0.4, 1.0)
    inverse_imag = jnp.clip(0.15 * jax.random.normal(keys[1], (H, BUSES), jnp.float32), -0.45, 0.45)
    lines = jnp.clip(0.17 * jax.random.normal(keys[2], (2, LINKS, H, BUSES), jnp.float32), -0.5, 0.5)
    inverse = jnp.stack([inverse_real, inverse_imag])[:, None]
    return jnp.concatenate([inverse, lines], axis=1).astype(jnp.float32)


def place_ends(array, rng, least, largest):
    shape = array.shape
    index_at = [jax.random.randint(jax.random.fold_in(rng, axis), (), 0, shape[axis]) for axis in range(len(shape))]
    array = array.at[tuple(index_at)].set(least)
    longest = shape.index(max(shape))
    index_at[longest] = (index_at[longest] + 1) % shape[longest]
    return array.at[tuple(index_at)].set(largest)


def levels(key, extent, pieces, least, high):
    def one(position, shards_of):
        heights = jax.random.uniform(jax.random.fold_in(jax.random.fold_in(key, 6), position), (shards_of,), jnp.float32, least / len(pieces), high / len(pieces))
        return jnp.repeat(jnp.exp(heights), extent[position] // shards_of).reshape((-1,) + (1,) * (len(extent) - position - 1))

    level = one(*pieces[0])
    for cut in pieces[1:]:
        level = level * one(*cut)
    return level


def centred(key, dims, scale, most, pieces=(), kind=jnp.bfloat16):
    drawn = scale * jax.random.normal(key, dims, jnp.float32)
    if pieces:
        drawn = drawn * levels(key, dims, pieces, -0.22, 0.18)
    return jnp.clip(drawn, -most, most).astype(kind)


def setup_inputs(seed: int = 0) -> dict:
    arg_keys = jax.random.split(jax.random.key(seed), 8)
    conv_volt = centred(arg_keys[0], (2, H, CONVS, S), 0.125, 0.75, ((2, 32),))
    conv_power = jnp.clip(jnp.exp(math.log(2.0) - 2.3025851 * jax.random.uniform(arg_keys[1], (CONVS, S), jnp.float32) ** levels(arg_keys[1], (CONVS, S), ((0, 32),), -0.2, 0.2)), 0.2, 2.0)
    conv_type = place_ends(jax.random.randint(arg_keys[2], (CONVS,), 0, TYPES), jax.random.fold_in(arg_keys[2], 1), 0, TYPES - 1).astype(jnp.int32)
    type_steep = jnp.clip(jax.random.uniform(arg_keys[3], (TYPES,), jnp.float32, 0.5, 4.0), 0.5, 4.0)
    conv_bus = draw_conv_bus(jax.random.fold_in(arg_keys[7], 71), 0)
    admittance = draw_admittance(jax.random.fold_in(arg_keys[7], 71), 0)
    link_offset = draw_link_offset(jax.random.fold_in(arg_keys[7], 71), 0)
    return {"conv_volt": conv_volt, "conv_power": conv_power, "conv_type": conv_type, "type_steep": type_steep, "conv_bus": conv_bus, "admittance": admittance, "link_offset": link_offset}


def make_basis():
    orders = jnp.arange(1, H + 1, dtype=jnp.int32)
    samples = jnp.arange(NT, dtype=jnp.int32)
    phases = ((orders[:, None] * samples[None, :]) % NT).astype(jnp.float32) * (2.0 * math.pi / NT)
    return jnp.concatenate([jnp.cos(phases), -jnp.sin(phases)], axis=0).astype(jnp.bfloat16)


def complex_product(left_real, left_imag, right_real, right_imag):
    return left_real * right_real - left_imag * right_imag, left_real * right_imag + left_imag * right_real


def reference(conv_volt, conv_power, conv_type, type_steep, conv_bus, admittance, link_offset):
    harmonic_basis = make_basis().astype(jnp.float32)
    steepness = type_steep[conv_type]
    volt_rows = conv_volt.reshape(2 * H, CONVS, S)

    def evaluate(group_num):
        first_row = (group_num * CONV_DEV).astype(jnp.int32)
        volt_group = lax.dynamic_slice_in_dim(volt_rows, first_row, CONV_DEV, 1).astype(jnp.float32)
        power_group = lax.dynamic_slice_in_dim(conv_power, first_row, CONV_DEV, 0)
        steep_group = lax.dynamic_slice_in_dim(steepness, first_row, CONV_DEV, 0)
        waveform = jnp.einsum("kcs,kn->csn", volt_group, harmonic_basis)
        current = (power_group[:, :, None] * jnp.tanh(steep_group[:, None, None] * waveform)).astype(jnp.bfloat16)
        spectra = jnp.einsum("csn,kn->kcs", current.astype(jnp.float32), harmonic_basis) * (NT ** -0.5)
        return spectra.astype(jnp.bfloat16)

    groups = lax.map(evaluate, jnp.arange(CONVS // CONV_DEV, dtype=jnp.int32))
    spectra = jnp.transpose(groups, (1, 0, 2, 3)).reshape(2, H, CONVS, S)
    bus_numbers = jnp.arange(BUSES, dtype=jnp.int32)

    def solve(harmonic):
        spectra_here = spectra[:, harmonic].astype(jnp.float32)
        summed = jnp.zeros((2, BUSES, S), jnp.float32).at[:, conv_bus, :].add(spectra_here)
        rounded = lax.optimization_barrier(summed.astype(jnp.bfloat16))
        inject_real = rounded[0].astype(jnp.float32)
        inject_imag = rounded[1].astype(jnp.float32)
        coeffs = admittance[:, :, harmonic]
        diag_real = coeffs[0, 0][:, None]
        diag_imag = coeffs[1, 0][:, None]
        volt_real, volt_imag = complex_product(diag_real, diag_imag, inject_real, inject_imag)
        for sweep_index in range(ITERS - 1):
            total_real, total_imag = inject_real, inject_imag
            for line_num in range(LINKS):
                target = bus_numbers + link_offset[line_num]
                inside = ((target >= 0) & (target < BUSES))[:, None]
                clipped = jnp.clip(target, 0, BUSES - 1)
                near_real = jnp.where(inside, volt_real[clipped], 0.0)
                near_imag = jnp.where(inside, volt_imag[clipped], 0.0)
                term_real, term_imag = complex_product(coeffs[0, 1 + line_num][:, None], coeffs[1, 1 + line_num][:, None], near_real, near_imag)
                total_real = total_real + term_real
                total_imag = total_imag + term_imag
            volt_real, volt_imag = complex_product(diag_real, diag_imag, total_real, total_imag)
        bus_here = jnp.stack([volt_real, volt_imag]).astype(jnp.bfloat16)
        return bus_here, bus_here[:, conv_bus, :]

    bus_all, conv_all = lax.map(solve, jnp.arange(H, dtype=jnp.int32))
    return jnp.transpose(bus_all, (1, 0, 2, 3)), jnp.transpose(conv_all, (1, 0, 2, 3))
```

```python
import functools
import math

import jax
import jax.numpy as jnp
import numpy as np
from jax import lax
from jax.experimental import pallas as pl
from jax.experimental.pallas import tpu as pltpu
from jax.sharding import PartitionSpec as P

NT = 1024
LANES = 128
CHUNKS = 4


def make_basis(orders):
    samples = np.arange(NT)
    phases = (np.arange(1, orders + 1)[:, None] * samples[None, :] % NT) * (2.0 * math.pi / NT)
    return np.concatenate([np.cos(phases), -np.sin(phases)], axis=0).astype(np.float32)


def kernel(
    nh,
    ny,
    near,
    volt_ref,
    power_ref,
    type_ref,
    steep_ref,
    bus_ref,
    adm_ref,
    off_ref,
    fwd_ref,
    inv_ref,
    perm_ref,
    back_ref,
    out_ref,
    next_ref,
    volts,
    send,
    recv,
    my_bus,
    buses,
    adm_side,
    off_side,
    weights,
    state,
    resp,
    send_back,
    result,
    spec_send,
    spec_recv,
    left_send,
    right_send,
    bus_send,
    bus_recv,
    bus_left,
    bus_right,
    side_send,
    side_recv,
    ret_send,
    ret_recv,
    local_sem,
    out_sem,
):
    me = lax.axis_index("harm")
    y = lax.axis_index("bus")
    hl = adm_ref.shape[2]
    block = adm_ref.shape[3]
    links = off_ref.shape[0]
    conv = power_ref.shape[0]
    sub = block // nh
    tiles = block // LANES + 1
    ext = tiles * LANES
    rows = 8 * (nh + 2)
    has_left = y > 0
    has_right = y < ny - 1

    barrier = pltpu.get_barrier_semaphore()

    def greet(d, by):
        pl.semaphore_signal(barrier, inc=1, device_id={"harm": d, "bus": by})

    def greet_peer(s, carry):
        greet(lax.rem(me + s, nh), y)
        return carry

    lax.fori_loop(1, nh, greet_peer, 0)

    @pl.when(has_left)
    def _():
        lax.fori_loop(0, nh, lambda d, c: (greet(d, y - 1), c)[1], 0)

    @pl.when(has_right)
    def _():
        lax.fori_loop(0, nh, lambda d, c: (greet(d, y + 1), c)[1], 0)

    span = volt_ref.shape[0] // conv
    per = LANES // conv
    for b in range(span // per):
        block_rows = jnp.dot(
            perm_ref[...], volt_ref[LANES * b : LANES * (b + 1), :], preferred_element_type=jnp.float32
        ).astype(jnp.bfloat16)
        for c in range(conv):
            volts[per * b : per * (b + 1), LANES * c : LANES * (c + 1)] = block_rows[per * c : per * (c + 1), :]
    steep = jnp.concatenate(
        [jnp.full((1, LANES), steep_ref[type_ref[c]], jnp.float32) for c in range(conv)], axis=1
    )
    power = jnp.concatenate([power_ref[c : c + 1, :] for c in range(conv)], axis=1) * NT ** (-0.5)
    part = NT // CHUNKS
    spectra = jnp.zeros((span, conv * LANES), jnp.float32)
    for q in range(CHUNKS):
        wave = jnp.dot(fwd_ref[part * q : part * (q + 1), :], volts[...], preferred_element_type=jnp.float32)
        now = jnp.tanh(steep * wave).astype(jnp.bfloat16)
        spectra = spectra + jnp.dot(
            inv_ref[:, part * q : part * (q + 1)], now, preferred_element_type=jnp.float32
        )
    spectra = (spectra * power).astype(jnp.bfloat16)
    per_dev = 8 * hl
    for b in range(span // per):
        stacked = jnp.concatenate(
            [spectra[per * b : per * (b + 1), LANES * c : LANES * (c + 1)] for c in range(conv)], axis=0
        )
        mixed = jnp.dot(back_ref[...], stacked, preferred_element_type=jnp.float32)
        count = LANES // per_dev
        send[count * b : count * (b + 1)] = mixed.reshape(count, hl, 8, LANES).astype(jnp.bfloat16)

    first = (y * nh + me) * sub
    row8 = lax.broadcasted_iota(jnp.int32, (8, LANES), 0) % conv
    numbers = jnp.zeros((8, LANES), jnp.float32)
    for c in range(conv):
        numbers = jnp.where(row8 == c, (bus_ref[c] - first).astype(jnp.float32), numbers)
    my_bus[...] = numbers.astype(jnp.bfloat16)

    @pl.when(jnp.logical_not(has_left))
    def _():
        recv[nh] = jnp.zeros(recv.shape[1:], recv.dtype)
        buses[nh] = jnp.zeros(buses.shape[1:], buses.dtype)
        adm_side[0] = jnp.zeros(adm_side.shape[1:], adm_side.dtype)
        off_side[0] = jnp.zeros(off_side.shape[1:], off_side.dtype)

    @pl.when(jnp.logical_not(has_right))
    def _():
        recv[nh + 1] = jnp.zeros(recv.shape[1:], recv.dtype)
        buses[nh + 1] = jnp.zeros(buses.shape[1:], buses.dtype)
        adm_side[1] = jnp.zeros(adm_side.shape[1:], adm_side.dtype)
        off_side[1] = jnp.zeros(off_side.shape[1:], off_side.dtype)

    pl.semaphore_wait(barrier, nh - 1 + nh * has_left.astype(jnp.int32) + nh * has_right.astype(jnp.int32))

    def remote(src, dst, send_sem, recv_sem, d, by):
        return pltpu.make_async_remote_copy(
            src_ref=src, dst_ref=dst, send_sem=send_sem, recv_sem=recv_sem, device_id={"harm": d, "bus": by}
        )

    def bus_copy(d, slot, by, sems):
        return remote(my_bus, buses.at[slot], sems.at[d], bus_recv.at[slot], d, by)

    def spec_copy(d, slot, by, sems):
        return remote(send.at[d], recv.at[slot], sems.at[d], spec_recv.at[slot], d, by)

    def ret_copy(d, source):
        place = next_ref.at[:, pl.ds(source * hl, hl)]
        return remote(send_back.at[d], place, ret_send.at[d], ret_recv.at[source], d, y)

    def side_copies(side):
        by = y + 1 if side == 0 else y - 1
        start = block - LANES if side == 0 else 0
        return (
            remote(
                adm_ref.at[:, :, :, pl.ds(start, LANES)],
                adm_side.at[side],
                side_send.at[side],
                side_recv.at[side],
                me,
                by,
            ),
            remote(
                off_ref.at[:, pl.ds(start, LANES)],
                off_side.at[side],
                side_send.at[2 + side],
                side_recv.at[2 + side],
                me,
                by,
            ),
        )

    send_right = jnp.logical_and(has_right, me == nh - 1)
    send_left = jnp.logical_and(has_left, me == 0)

    def each(low, body):
        def step(i, carry):
            body(i)
            return carry

        lax.fori_loop(low, nh, step, 0)

    def peer(s):
        return lax.rem(me + s, nh)

    each(1, lambda s: bus_copy(peer(s), me, y, bus_send).start())

    @pl.when(send_right)
    def _():
        each(0, lambda d: bus_copy(d, nh, y + 1, bus_right).start())

    @pl.when(send_left)
    def _():
        each(0, lambda d: bus_copy(d, nh + 1, y - 1, bus_left).start())

    @pl.when(has_right)
    def _():
        for copy in side_copies(0):
            copy.start()

    @pl.when(has_left)
    def _():
        for copy in side_copies(1):
            copy.start()

    each(1, lambda s: spec_copy(peer(s), me, y, spec_send).start())

    @pl.when(send_right)
    def _():
        each(0, lambda d: spec_copy(d, nh, y + 1, left_send).start())

    @pl.when(send_left)
    def _():
        each(0, lambda d: spec_copy(d, nh + 1, y - 1, right_send).start())

    recv[me] = send[me]
    buses[me] = my_bus[...]

    @pl.when(has_left)
    def _():
        for copy in side_copies(0):
            copy.wait_recv()

    @pl.when(has_right)
    def _():
        for copy in side_copies(1):
            copy.wait_recv()

    lane = lax.broadcasted_iota(jnp.int32, (1, LANES), 1)
    is_right = lane < LANES // 2

    def adm_row(p, k, h, t):
        if t < tiles - 1:
            return adm_ref[p, k, h : h + 1, LANES * t : LANES * (t + 1)]
        return jnp.where(is_right, adm_side[1, p, k, h : h + 1, :], adm_side[0, p, k, h : h + 1, :])

    def off_row(k, t):
        if t < tiles - 1:
            return off_ref[k : k + 1, LANES * t : LANES * (t + 1)]
        return jnp.where(is_right, off_side[1, k : k + 1, :], off_side[0, k : k + 1, :])

    low, high = LANES - 16, 2 * LANES + 16
    band = lax.broadcasted_iota(jnp.int32, (high - low, LANES), 0) + low
    for t in range(tiles):
        masks = [band == lane + LANES + off_row(k, t) for k in range(links)]
        for h in range(hl):
            d_real, d_imag = adm_row(0, 0, h, t), adm_row(1, 0, h, t)
            total_real = jnp.zeros(band.shape, jnp.float32)
            total_imag = jnp.zeros(band.shape, jnp.float32)
            for k in range(links):
                l_real, l_imag = adm_row(0, 1 + k, h, t), adm_row(1, 1 + k, h, t)
                total_real += jnp.where(masks[k], d_real * l_real - d_imag * l_imag, 0.0)
                total_imag += jnp.where(masks[k], d_real * l_imag + d_imag * l_real, 0.0)
            blank = jnp.zeros((low, 2 * LANES), jnp.bfloat16)
            weights[h, t, 0:low, :] = blank
            weights[h, t, high:, :] = blank
            weights[h, t, low:high, 0:LANES] = total_real.astype(jnp.bfloat16)
            weights[h, t, low:high, LANES:] = total_imag.astype(jnp.bfloat16)

    each(1, lambda s: bus_copy(peer(s), peer(s), y, bus_send).wait_recv())

    @pl.when(has_left)
    def _():
        bus_copy(0, nh, y, bus_send).wait_recv()

    @pl.when(has_right)
    def _():
        bus_copy(0, nh + 1, y, bus_send).wait_recv()

    row = lax.broadcasted_iota(jnp.int32, (rows, LANES), 0)
    slot = row // 8
    is_real = row % 8 < conv
    base = jnp.where(slot == nh, ext - sub, jnp.where(slot == nh + 1, block, slot * sub))
    at_bus = base + buses[...].astype(jnp.float32).reshape(rows, LANES).astype(jnp.int32)
    hits = [at_bus == lane + LANES * t for t in range(tiles)]
    own = 8 * nh
    pick_real = [
        jnp.where(jnp.logical_and(hits[t], is_real), 1.0, 0.0)[:own].astype(jnp.bfloat16) for t in range(tiles - 1)
    ]
    pick_imag = [
        jnp.where(jnp.logical_and(hits[t], jnp.logical_not(is_real)), 1.0, 0.0)[:own].astype(jnp.bfloat16)
        for t in range(tiles - 1)
    ]
    for h in range(hl):
        start_real, start_imag = [], []
        for t in range(tiles):
            d_real, d_imag = adm_row(0, 0, h, t), adm_row(1, 0, h, t)
            start_real.append(jnp.where(hits[t], jnp.where(is_real, d_real, -d_imag), 0.0))
            start_imag.append(jnp.where(hits[t], jnp.where(is_real, d_imag, d_real), 0.0))
        now_real, now_imag = start_real, start_imag
        for last in (False, True):
            for t in range(tiles):
                state[0:rows, LANES * t : LANES * (t + 1)] = now_real[t].astype(jnp.bfloat16)
                state[rows:, LANES * t : LANES * (t + 1)] = now_imag[t].astype(jnp.bfloat16)
            new_real, new_imag = [], []
            for t in range(tiles - 1 if last else tiles):
                around = jnp.concatenate(
                    [
                        state[:, LANES * j : LANES * (j + 1)]
                        for j in ((t - 1) % tiles, t, (t + 1) % tiles)
                    ],
                    axis=1,
                )
                both = jnp.dot(around, weights[h, t], preferred_element_type=jnp.float32)
                new_real.append(start_real[t] + both[:rows, :LANES] - both[rows:, LANES:])
                new_imag.append(start_imag[t] + both[:rows, LANES:] + both[rows:, :LANES])
            now_real, now_imag = new_real, new_imag
        chosen = jnp.zeros((own, rows), jnp.float32)
        for t in range(tiles - 1):
            real_t = now_real[t].T.astype(jnp.bfloat16)
            imag_t = now_imag[t].T.astype(jnp.bfloat16)
            resp[h, own + LANES * t : own + LANES * (t + 1), :] = real_t
            resp[h, own + block + LANES * t : own + block + LANES * (t + 1), :] = imag_t
            chosen += jnp.dot(pick_real[t], real_t, preferred_element_type=jnp.float32)
            chosen += jnp.dot(pick_imag[t], imag_t, preferred_element_type=jnp.float32)
        resp[h, 0:own, :] = chosen.astype(jnp.bfloat16)

    each(1, lambda s: spec_copy(peer(s), peer(s), y, spec_send).wait_recv())

    @pl.when(has_left)
    def _():
        spec_copy(0, nh, y, spec_send).wait_recv()

    @pl.when(has_right)
    def _():
        spec_copy(0, nh + 1, y, spec_send).wait_recv()

    arrived = []
    for h in range(hl):
        arrived.append(recv[:, h].astype(jnp.float32).reshape(rows, LANES).astype(jnp.bfloat16))
        at_conv = jnp.dot(resp[h, 0:own, :], arrived[h], preferred_element_type=jnp.float32)
        at_conv = at_conv.reshape(nh, 2, conv, LANES).astype(jnp.bfloat16)
        send_back[:, :, h] = at_conv
    each(1, lambda s: ret_copy(peer(s), me).start())
    keep = pltpu.make_async_copy(send_back.at[me], next_ref.at[:, pl.ds(me * hl, hl)], local_sem)
    keep.start()
    outs = []
    for h in range(hl):
        solved = jnp.dot(resp[h, own:, :], arrived[h], preferred_element_type=jnp.float32)
        result[:, h] = solved.astype(jnp.bfloat16).reshape(2, block, LANES)
        copy = pltpu.make_async_copy(result.at[:, h], out_ref.at[:, h], out_sem.at[h])
        copy.start()
        outs.append(copy)

    each(1, lambda s: bus_copy(peer(s), me, y, bus_send).wait_send())
    each(1, lambda s: spec_copy(peer(s), me, y, spec_send).wait_send())

    @pl.when(has_right)
    def _():
        for copy in side_copies(0):
            copy.wait_send()

    @pl.when(has_left)
    def _():
        for copy in side_copies(1):
            copy.wait_send()

    @pl.when(send_right)
    def _():
        each(0, lambda d: bus_copy(d, nh, y + 1, bus_right).wait_send())
        each(0, lambda d: spec_copy(d, nh, y + 1, left_send).wait_send())

    @pl.when(send_left)
    def _():
        each(0, lambda d: bus_copy(d, nh + 1, y - 1, bus_left).wait_send())
        each(0, lambda d: spec_copy(d, nh + 1, y - 1, right_send).wait_send())

    keep.wait()
    for copy in outs:
        copy.wait()
    each(1, lambda s: ret_copy(peer(s), me).wait_send())
    each(1, lambda s: ret_copy(peer(s), peer(s)).wait_recv())


def local(nh, ny, conv_volt, conv_power, conv_type, type_steep, conv_bus, admittance, link_offset):
    _, orders, conv, snaps = conv_volt.shape
    hl = orders // nh
    block = admittance.shape[3]
    tiles = block // LANES + 1
    rows = 8 * (nh + 2)
    span = 2 * orders
    basis = make_basis(orders)
    regrouped = basis.reshape(2, orders, NT).transpose(1, 0, 2).reshape(span, NT)
    per = LANES // conv
    perm = np.zeros((LANES, LANES), np.float32)
    for c in range(conv):
        for k in range(per):
            perm[per * c + k, conv * k + c] = 1.0
    vmem = pl.BlockSpec(memory_space=pltpu.VMEM)
    smem = pl.BlockSpec(memory_space=pltpu.SMEM)
    anywhere = pl.BlockSpec(memory_space=pl.ANY)
    bf16 = jnp.bfloat16
    dma = pltpu.SemaphoreType.DMA
    return pl.pallas_call(
        functools.partial(kernel, nh, ny, None),
        out_shape=(
            jax.ShapeDtypeStruct((2, hl, block, snaps), bf16),
            jax.ShapeDtypeStruct((2, orders, conv, snaps), bf16),
        ),
        in_specs=[vmem, vmem, smem, smem, smem, vmem, vmem, vmem, vmem, vmem, vmem],
        out_specs=(anywhere, anywhere),
        scratch_shapes=[
            pltpu.VMEM((span, conv * LANES), bf16),
            pltpu.VMEM((nh, hl, 8, LANES), bf16),
            pltpu.VMEM((nh + 2, hl, 8, LANES), bf16),
            pltpu.VMEM((8, LANES), bf16),
            pltpu.VMEM((nh + 2, 8, LANES), bf16),
            pltpu.VMEM((2,) + admittance.shape[:3] + (LANES,), jnp.float32),
            pltpu.VMEM((2, link_offset.shape[0], LANES), jnp.int32),
            pltpu.VMEM((hl, tiles, 3 * LANES, 2 * LANES), bf16),
            pltpu.VMEM((2 * rows, tiles * LANES), bf16),
            pltpu.VMEM((hl, 8 * nh + 2 * block, rows), bf16),
            pltpu.VMEM((nh, 2, hl, conv, LANES), bf16),
            pltpu.VMEM((2, hl, block, LANES), bf16),
            dma((nh,)),
            dma((nh + 2,)),
            dma((nh,)),
            dma((nh,)),
            dma((nh,)),
            dma((nh + 2,)),
            dma((nh,)),
            dma((nh,)),
            dma((4,)),
            dma((4,)),
            dma((nh,)),
            dma((nh,)),
            dma,
            dma((hl,)),
        ],
        compiler_params=pltpu.CompilerParams(collective_id=0, has_side_effects=True, vmem_limit_bytes=56 * 2**20),
        name="power_flow",
    )(
        conv_volt.reshape(span * conv, snaps),
        conv_power,
        conv_type,
        type_steep,
        conv_bus,
        admittance,
        link_offset,
        jnp.asarray(basis.T, bf16),
        jnp.asarray(regrouped, bf16),
        jnp.asarray(perm, bf16),
        jnp.asarray(perm.T, bf16),
    )


def solution(mesh):
    in_specs = (
        P(None, None, ("bus", "harm"), None),
        P(("bus", "harm"), None),
        P(("bus", "harm")),
        P(),
        P(("bus", "harm")),
        P(None, None, "harm", "bus"),
        P(None, "bus"),
    )
    out_specs = (P(None, "harm", "bus", None), P(None, None, ("bus", "harm"), None))
    body = functools.partial(local, mesh.shape["harm"], mesh.shape["bus"])
    return jax.shard_map(body, mesh=mesh, in_specs=in_specs, out_specs=out_specs, check_vma=False)
```

```python
import functools
import math

import jax
import jax.numpy as jnp
import numpy as np
from jax import lax
from jax.experimental import pallas as pl
from jax.experimental.pallas import tpu as pltpu
from jax.sharding import PartitionSpec as P

NT = 1024
LANES = 128
CHUNKS = 4


def make_basis(orders):
    samples = np.arange(NT)
    phases = (np.arange(1, orders + 1)[:, None] * samples[None, :] % NT) * (2.0 * math.pi / NT)
    return np.concatenate([np.cos(phases), -np.sin(phases)], axis=0).astype(np.float32)


def kernel(
    nh,
    ny,
    volt_ref,
    power_ref,
    type_ref,
    steep_ref,
    bus_ref,
    adm_ref,
    off_ref,
    fwd_ref,
    inv_ref,
    perm_ref,
    back_ref,
    out_ref,
    next_ref,
    volts,
    send,
    recv,
    my_bus,
    buses,
    adm_side,
    off_side,
    weights,
    state,
    resp,
    send_back,
    spec_send,
    spec_recv,
    left_send,
    right_send,
    bus_send,
    bus_recv,
    bus_left,
    bus_right,
    side_send,
    side_recv,
    ret_send,
    ret_recv,
    local_sem,
):
    me = lax.axis_index("harm")
    y = lax.axis_index("bus")
    hl = adm_ref.shape[2]
    block = adm_ref.shape[3]
    links = off_ref.shape[0]
    conv = power_ref.shape[0]
    sub = block // nh
    tiles = block // LANES + 1
    ext = tiles * LANES
    rows = 8 * (nh + 2)
    has_left = y > 0
    has_right = y < ny - 1

    barrier = pltpu.get_barrier_semaphore()

    def greet(d, by):
        pl.semaphore_signal(barrier, inc=1, device_id={"harm": d, "bus": by})

    def greet_peer(s, carry):
        greet(lax.rem(me + s, nh), y)
        return carry

    lax.fori_loop(1, nh, greet_peer, 0)

    @pl.when(has_left)
    def _():
        lax.fori_loop(0, nh, lambda d, c: (greet(d, y - 1), c)[1], 0)

    @pl.when(has_right)
    def _():
        lax.fori_loop(0, nh, lambda d, c: (greet(d, y + 1), c)[1], 0)

    span = volt_ref.shape[0] // conv
    per = LANES // conv
    for b in range(span // per):
        block_rows = jnp.dot(
            perm_ref[...], volt_ref[LANES * b : LANES * (b + 1), :], preferred_element_type=jnp.float32
        ).astype(jnp.bfloat16)
        for c in range(conv):
            volts[per * b : per * (b + 1), LANES * c : LANES * (c + 1)] = block_rows[per * c : per * (c + 1), :]
    steep = jnp.concatenate(
        [jnp.full((1, LANES), steep_ref[type_ref[c]], jnp.float32) for c in range(conv)], axis=1
    )
    power = jnp.concatenate([power_ref[c : c + 1, :] for c in range(conv)], axis=1) * NT ** (-0.5)
    part = NT // CHUNKS
    spectra = jnp.zeros((span, conv * LANES), jnp.float32)
    for q in range(CHUNKS):
        wave = jnp.dot(fwd_ref[part * q : part * (q + 1), :], volts[...], preferred_element_type=jnp.float32)
        now = jnp.tanh(steep * wave).astype(jnp.bfloat16)
        spectra = spectra + jnp.dot(
            inv_ref[:, part * q : part * (q + 1)], now, preferred_element_type=jnp.float32
        )
    spectra = (spectra * power).astype(jnp.bfloat16)
    per_dev = 8 * hl
    for b in range(span // per):
        stacked = jnp.concatenate(
            [spectra[per * b : per * (b + 1), LANES * c : LANES * (c + 1)] for c in range(conv)], axis=0
        )
        mixed = jnp.dot(back_ref[...], stacked, preferred_element_type=jnp.float32)
        count = LANES // per_dev
        send[count * b : count * (b + 1)] = mixed.reshape(count, hl, 8, LANES).astype(jnp.bfloat16)

    first = (y * nh + me) * sub
    row8 = lax.broadcasted_iota(jnp.int32, (8, LANES), 0) % conv
    numbers = jnp.zeros((8, LANES), jnp.float32)
    for c in range(conv):
        numbers = jnp.where(row8 == c, (bus_ref[c] - first).astype(jnp.float32), numbers)
    my_bus[...] = numbers.astype(jnp.bfloat16)

    @pl.when(jnp.logical_not(has_left))
    def _():
        recv[nh] = jnp.zeros(recv.shape[1:], recv.dtype)
        buses[nh] = jnp.zeros(buses.shape[1:], buses.dtype)
        adm_side[0] = jnp.zeros(adm_side.shape[1:], adm_side.dtype)
        off_side[0] = jnp.zeros(off_side.shape[1:], off_side.dtype)

    @pl.when(jnp.logical_not(has_right))
    def _():
        recv[nh + 1] = jnp.zeros(recv.shape[1:], recv.dtype)
        buses[nh + 1] = jnp.zeros(buses.shape[1:], buses.dtype)
        adm_side[1] = jnp.zeros(adm_side.shape[1:], adm_side.dtype)
        off_side[1] = jnp.zeros(off_side.shape[1:], off_side.dtype)

    pl.semaphore_wait(barrier, nh - 1 + nh * has_left.astype(jnp.int32) + nh * has_right.astype(jnp.int32))

    def remote(src, dst, send_sem, recv_sem, d, by):
        return pltpu.make_async_remote_copy(
            src_ref=src, dst_ref=dst, send_sem=send_sem, recv_sem=recv_sem, device_id={"harm": d, "bus": by}
        )

    def bus_copy(d, slot, by, sems):
        return remote(my_bus, buses.at[slot], sems.at[d], bus_recv.at[slot], d, by)

    def spec_copy(d, slot, by, sems):
        return remote(send.at[d], recv.at[slot], sems.at[d], spec_recv.at[slot], d, by)

    def ret_copy(d, source):
        place = next_ref.at[:, pl.ds(source * hl, hl)]
        return remote(send_back.at[d], place, ret_send.at[d], ret_recv.at[source], d, y)

    def side_copies(side):
        by = y + 1 if side == 0 else y - 1
        start = block - LANES if side == 0 else 0
        return (
            remote(
                adm_ref.at[:, :, :, pl.ds(start, LANES)],
                adm_side.at[side],
                side_send.at[side],
                side_recv.at[side],
                me,
                by,
            ),
            remote(
                off_ref.at[:, pl.ds(start, LANES)],
                off_side.at[side],
                side_send.at[2 + side],
                side_recv.at[2 + side],
                me,
                by,
            ),
        )

    send_right = jnp.logical_and(has_right, me == nh - 1)
    send_left = jnp.logical_and(has_left, me == 0)

    def each(low, body):
        def step(i, carry):
            body(i)
            return carry

        lax.fori_loop(low, nh, step, 0)

    def peer(s):
        return lax.rem(me + s, nh)

    each(1, lambda s: bus_copy(peer(s), me, y, bus_send).start())

    @pl.when(send_right)
    def _():
        each(0, lambda d: bus_copy(d, nh, y + 1, bus_right).start())

    @pl.when(send_left)
    def _():
        each(0, lambda d: bus_copy(d, nh + 1, y - 1, bus_left).start())

    @pl.when(has_right)
    def _():
        for copy in side_copies(0):
            copy.start()

    @pl.when(has_left)
    def _():
        for copy in side_copies(1):
            copy.start()

    each(1, lambda s: spec_copy(peer(s), me, y, spec_send).start())

    @pl.when(send_right)
    def _():
        each(0, lambda d: spec_copy(d, nh, y + 1, left_send).start())

    @pl.when(send_left)
    def _():
        each(0, lambda d: spec_copy(d, nh + 1, y - 1, right_send).start())

    recv[me] = send[me]
    buses[me] = my_bus[...]

    @pl.when(has_left)
    def _():
        for copy in side_copies(0):
            copy.wait_recv()

    @pl.when(has_right)
    def _():
        for copy in side_copies(1):
            copy.wait_recv()

    lane = lax.broadcasted_iota(jnp.int32, (1, LANES), 1)
    is_right = lane < LANES // 2

    def adm_row(p, k, h, t):
        if t < tiles - 1:
            return adm_ref[p, k, h : h + 1, LANES * t : LANES * (t + 1)]
        return jnp.where(is_right, adm_side[1, p, k, h : h + 1, :], adm_side[0, p, k, h : h + 1, :])

    def off_row(k, t):
        if t < tiles - 1:
            return off_ref[k : k + 1, LANES * t : LANES * (t + 1)]
        return jnp.where(is_right, off_side[1, k : k + 1, :], off_side[0, k : k + 1, :])

    low, high = LANES - 16, 2 * LANES + 16
    band = lax.broadcasted_iota(jnp.int32, (high - low, LANES), 0) + low
    for t in range(tiles):
        masks = [band == lane + LANES + off_row(k, t) for k in range(links)]
        for h in range(hl):
            d_real, d_imag = adm_row(0, 0, h, t), adm_row(1, 0, h, t)
            total_real = jnp.zeros(band.shape, jnp.float32)
            total_imag = jnp.zeros(band.shape, jnp.float32)
            for k in range(links):
                l_real, l_imag = adm_row(0, 1 + k, h, t), adm_row(1, 1 + k, h, t)
                total_real += jnp.where(masks[k], d_real * l_real - d_imag * l_imag, 0.0)
                total_imag += jnp.where(masks[k], d_real * l_imag + d_imag * l_real, 0.0)
            blank = jnp.zeros((low, 2 * LANES), jnp.bfloat16)
            weights[h, t, 0:low, :] = blank
            weights[h, t, high:, :] = blank
            weights[h, t, low:high, 0:LANES] = total_real.astype(jnp.bfloat16)
            weights[h, t, low:high, LANES:] = total_imag.astype(jnp.bfloat16)

    each(1, lambda s: bus_copy(peer(s), peer(s), y, bus_send).wait_recv())

    @pl.when(has_left)
    def _():
        bus_copy(0, nh, y, bus_send).wait_recv()

    @pl.when(has_right)
    def _():
        bus_copy(0, nh + 1, y, bus_send).wait_recv()

    row = lax.broadcasted_iota(jnp.int32, (rows, LANES), 0)
    slot = row // 8
    is_real = row % 8 < conv
    base = jnp.where(slot == nh, ext - sub, jnp.where(slot == nh + 1, block, slot * sub))
    at_bus = base + buses[...].astype(jnp.float32).reshape(rows, LANES).astype(jnp.int32)
    hits = [at_bus == lane + LANES * t for t in range(tiles)]
    own = 8 * nh
    pick_real = [
        jnp.where(jnp.logical_and(hits[t], is_real), 1.0, 0.0)[:own].astype(jnp.bfloat16) for t in range(tiles - 1)
    ]
    pick_imag = [
        jnp.where(jnp.logical_and(hits[t], jnp.logical_not(is_real)), 1.0, 0.0)[:own].astype(jnp.bfloat16)
        for t in range(tiles - 1)
    ]
    for h in range(hl):
        start_real, start_imag = [], []
        for t in range(tiles):
            d_real, d_imag = adm_row(0, 0, h, t), adm_row(1, 0, h, t)
            start_real.append(jnp.where(hits[t], jnp.where(is_real, d_real, -d_imag), 0.0))
            start_imag.append(jnp.where(hits[t], jnp.where(is_real, d_imag, d_real), 0.0))
        now_real, now_imag = start_real, start_imag
        for last in (False, True):
            for t in range(tiles):
                state[0:rows, LANES * t : LANES * (t + 1)] = now_real[t].astype(jnp.bfloat16)
                state[rows:, LANES * t : LANES * (t + 1)] = now_imag[t].astype(jnp.bfloat16)
            new_real, new_imag = [], []
            for t in range(tiles - 1 if last else tiles):
                around = jnp.concatenate(
                    [
                        state[:, LANES * j : LANES * (j + 1)]
                        for j in ((t - 1) % tiles, t, (t + 1) % tiles)
                    ],
                    axis=1,
                )
                both = jnp.dot(around, weights[h, t], preferred_element_type=jnp.float32)
                new_real.append(start_real[t] + both[:rows, :LANES] - both[rows:, LANES:])
                new_imag.append(start_imag[t] + both[:rows, LANES:] + both[rows:, :LANES])
            now_real, now_imag = new_real, new_imag
        chosen = jnp.zeros((own, rows), jnp.float32)
        for t in range(tiles - 1):
            real_t = now_real[t].T.astype(jnp.bfloat16)
            imag_t = now_imag[t].T.astype(jnp.bfloat16)
            resp[h, own + LANES * t : own + LANES * (t + 1), :] = real_t
            resp[h, own + block + LANES * t : own + block + LANES * (t + 1), :] = imag_t
            chosen += jnp.dot(pick_real[t], real_t, preferred_element_type=jnp.float32)
            chosen += jnp.dot(pick_imag[t], imag_t, preferred_element_type=jnp.float32)
        resp[h, 0:own, :] = chosen.astype(jnp.bfloat16)

    each(1, lambda s: spec_copy(peer(s), peer(s), y, spec_send).wait_recv())

    @pl.when(has_left)
    def _():
        spec_copy(0, nh, y, spec_send).wait_recv()

    @pl.when(has_right)
    def _():
        spec_copy(0, nh + 1, y, spec_send).wait_recv()

    arrived = []
    for h in range(hl):
        arrived.append(recv[:, h].astype(jnp.float32).reshape(rows, LANES).astype(jnp.bfloat16))
        at_conv = jnp.dot(resp[h, 0:own, :], arrived[h], preferred_element_type=jnp.float32)
        at_conv = at_conv.reshape(nh, 2, conv, LANES).astype(jnp.bfloat16)
        send_back[:, :, h] = at_conv
    each(1, lambda s: ret_copy(peer(s), me).start())
    keep = pltpu.make_async_copy(send_back.at[me], next_ref.at[:, pl.ds(me * hl, hl)], local_sem)
    keep.start()
    for h in range(hl):
        solved = jnp.dot(resp[h, own:, :], arrived[h], preferred_element_type=jnp.float32)
        out_ref[:, h] = solved.astype(jnp.bfloat16).reshape(2, block, LANES)

    each(1, lambda s: bus_copy(peer(s), me, y, bus_send).wait_send())
    each(1, lambda s: spec_copy(peer(s), me, y, spec_send).wait_send())

    @pl.when(has_right)
    def _():
        for copy in side_copies(0):
            copy.wait_send()

    @pl.when(has_left)
    def _():
        for copy in side_copies(1):
            copy.wait_send()

    @pl.when(send_right)
    def _():
        each(0, lambda d: bus_copy(d, nh, y + 1, bus_right).wait_send())
        each(0, lambda d: spec_copy(d, nh, y + 1, left_send).wait_send())

    @pl.when(send_left)
    def _():
        each(0, lambda d: bus_copy(d, nh + 1, y - 1, bus_left).wait_send())
        each(0, lambda d: spec_copy(d, nh + 1, y - 1, right_send).wait_send())

    keep.wait()
    each(1, lambda s: ret_copy(peer(s), me).wait_send())
    each(1, lambda s: ret_copy(peer(s), peer(s)).wait_recv())


def store(volt_ref, next_ref, volt_out, next_out, sems):
    copies = [pltpu.make_async_copy(volt_ref.at[p], volt_out.at[p], sems.at[p]) for p in range(2)]
    copies.append(pltpu.make_async_copy(next_ref, next_out, sems.at[2]))
    for copy in copies:
        copy.start()
    for copy in copies:
        copy.wait()


def local(nh, ny, conv_volt, conv_power, conv_type, type_steep, conv_bus, admittance, link_offset):
    _, orders, conv, snaps = conv_volt.shape
    hl = orders // nh
    block = admittance.shape[3]
    tiles = block // LANES + 1
    rows = 8 * (nh + 2)
    span = 2 * orders
    basis = make_basis(orders)
    regrouped = basis.reshape(2, orders, NT).transpose(1, 0, 2).reshape(span, NT)
    per = LANES // conv
    perm = np.zeros((LANES, LANES), np.float32)
    for c in range(conv):
        for k in range(per):
            perm[per * c + k, conv * k + c] = 1.0
    vmem = pl.BlockSpec(memory_space=pltpu.VMEM)
    smem = pl.BlockSpec(memory_space=pltpu.SMEM)
    anywhere = pl.BlockSpec(memory_space=pl.ANY)
    bf16 = jnp.bfloat16
    dma = pltpu.SemaphoreType.DMA
    volt_shape, next_shape = (2, hl, block, snaps), (2, orders, conv, snaps)
    solved = pl.pallas_call(
        functools.partial(kernel, nh, ny),
        out_shape=(pltpu.VMEM(volt_shape, bf16), pltpu.VMEM(next_shape, bf16)),
        in_specs=[vmem, vmem, smem, smem, smem, vmem, vmem, vmem, vmem, vmem, vmem],
        out_specs=(vmem, vmem),
        scratch_shapes=[
            pltpu.VMEM((span, conv * LANES), bf16),
            pltpu.VMEM((nh, hl, 8, LANES), bf16),
            pltpu.VMEM((nh + 2, hl, 8, LANES), bf16),
            pltpu.VMEM((8, LANES), bf16),
            pltpu.VMEM((nh + 2, 8, LANES), bf16),
            pltpu.VMEM((2,) + admittance.shape[:3] + (LANES,), jnp.float32),
            pltpu.VMEM((2, link_offset.shape[0], LANES), jnp.int32),
            pltpu.VMEM((hl, tiles, 3 * LANES, 2 * LANES), bf16),
            pltpu.VMEM((2 * rows, tiles * LANES), bf16),
            pltpu.VMEM((hl, 8 * nh + 2 * block, rows), bf16),
            pltpu.VMEM((nh, 2, hl, conv, LANES), bf16),
            dma((nh,)),
            dma((nh + 2,)),
            dma((nh,)),
            dma((nh,)),
            dma((nh,)),
            dma((nh + 2,)),
            dma((nh,)),
            dma((nh,)),
            dma((4,)),
            dma((4,)),
            dma((nh,)),
            dma((nh,)),
            dma,
        ],
        compiler_params=pltpu.CompilerParams(collective_id=0, has_side_effects=True, vmem_limit_bytes=56 * 2**20),
        name="power_flow",
    )(
        conv_volt.reshape(span * conv, snaps),
        conv_power,
        conv_type,
        type_steep,
        conv_bus,
        admittance,
        link_offset,
        jnp.asarray(basis.T, bf16),
        jnp.asarray(regrouped, bf16),
        jnp.asarray(perm, bf16),
        jnp.asarray(perm.T, bf16),
    )
    return pl.pallas_call(
        store,
        out_shape=(jax.ShapeDtypeStruct(volt_shape, bf16), jax.ShapeDtypeStruct(next_shape, bf16)),
        in_specs=[vmem, vmem],
        out_specs=(anywhere, anywhere),
        scratch_shapes=[dma((3,))],
        compiler_params=pltpu.CompilerParams(vmem_limit_bytes=32 * 2**20),
        name="store_results",
    )(*solved)


def solution(mesh):
    in_specs = (
        P(None, None, ("bus", "harm"), None),
        P(("bus", "harm"), None),
        P(("bus", "harm")),
        P(),
        P(("bus", "harm")),
        P(None, None, "harm", "bus"),
        P(None, "bus"),
    )
    out_specs = (P(None, "harm", "bus", None), P(None, None, ("bus", "harm"), None))
    body = functools.partial(local, mesh.shape["harm"], mesh.shape["bus"])
    return jax.shard_map(body, mesh=mesh, in_specs=in_specs, out_specs=out_specs, check_vma=False)
```

```python
import functools
import math

import jax
import jax.numpy as jnp
import numpy as np
from jax import lax
from jax.experimental import pallas as pl
from jax.experimental.pallas import tpu as pltpu
from jax.sharding import PartitionSpec as P

NT = 1024
LANES = 128
CHUNKS = 4


def make_basis(orders):
    samples = np.arange(NT)
    phases = (np.arange(1, orders + 1)[:, None] * samples[None, :] % NT) * (2.0 * math.pi / NT)
    return np.concatenate([np.cos(phases), -np.sin(phases)], axis=0).astype(np.float32)


def kernel(
    nh,
    ny,
    volt_ref,
    power_ref,
    type_ref,
    steep_ref,
    bus_ref,
    adm_ref,
    off_ref,
    fwd_ref,
    inv_ref,
    perm_ref,
    back_ref,
    out_ref,
    next_ref,
    volts,
    send,
    recv,
    my_bus,
    buses,
    adm_side,
    off_side,
    weights,
    resp,
    send_back,
    spec_send,
    spec_recv,
    left_send,
    right_send,
    bus_send,
    bus_recv,
    bus_left,
    bus_right,
    side_send,
    side_recv,
    ret_send,
    ret_recv,
    local_sem,
):
    me = lax.axis_index("harm")
    y = lax.axis_index("bus")
    hl = adm_ref.shape[2]
    block = adm_ref.shape[3]
    links = off_ref.shape[0]
    conv = power_ref.shape[0]
    sub = block // nh
    tiles = block // LANES
    around = LANES // sub
    rows = 8 * (around + 2)
    has_left = y > 0
    has_right = y < ny - 1

    barrier = pltpu.get_barrier_semaphore()

    def greet(d, by):
        pl.semaphore_signal(barrier, inc=1, device_id={"harm": d, "bus": by})

    def greet_peer(s, carry):
        greet(lax.rem(me + s, nh), y)
        return carry

    lax.fori_loop(1, nh, greet_peer, 0)

    @pl.when(has_left)
    def _():
        lax.fori_loop(0, nh, lambda d, c: (greet(d, y - 1), c)[1], 0)

    @pl.when(has_right)
    def _():
        lax.fori_loop(0, nh, lambda d, c: (greet(d, y + 1), c)[1], 0)

    span = volt_ref.shape[0] // conv
    per = LANES // conv
    for b in range(span // per):
        block_rows = jnp.dot(
            perm_ref[...], volt_ref[LANES * b : LANES * (b + 1), :], preferred_element_type=jnp.float32
        ).astype(jnp.bfloat16)
        for c in range(conv):
            volts[per * b : per * (b + 1), LANES * c : LANES * (c + 1)] = block_rows[per * c : per * (c + 1), :]
    steep = jnp.concatenate(
        [jnp.full((1, LANES), steep_ref[type_ref[c]], jnp.float32) for c in range(conv)], axis=1
    )
    power = jnp.concatenate([power_ref[c : c + 1, :] for c in range(conv)], axis=1) * NT ** (-0.5)
    part = NT // CHUNKS
    spectra = jnp.zeros((span, conv * LANES), jnp.float32)
    for q in range(CHUNKS):
        wave = jnp.dot(fwd_ref[part * q : part * (q + 1), :], volts[...], preferred_element_type=jnp.float32)
        now = jnp.tanh(steep * wave).astype(jnp.bfloat16)
        spectra = spectra + jnp.dot(
            inv_ref[:, part * q : part * (q + 1)], now, preferred_element_type=jnp.float32
        )
    spectra = (spectra * power).astype(jnp.bfloat16)
    per_dev = 8 * hl
    for b in range(span // per):
        stacked = jnp.concatenate(
            [spectra[per * b : per * (b + 1), LANES * c : LANES * (c + 1)] for c in range(conv)], axis=0
        )
        mixed = jnp.dot(back_ref[...], stacked, preferred_element_type=jnp.float32)
        count = LANES // per_dev
        send[count * b : count * (b + 1)] = mixed.reshape(count, hl, 8, LANES).astype(jnp.bfloat16)

    first = (y * nh + me) * sub
    row8 = lax.broadcasted_iota(jnp.int32, (8, LANES), 0) % conv
    numbers = jnp.zeros((8, LANES), jnp.float32)
    for c in range(conv):
        numbers = jnp.where(row8 == c, (bus_ref[c] - first).astype(jnp.float32), numbers)
    my_bus[...] = numbers.astype(jnp.bfloat16)

    @pl.when(jnp.logical_not(has_left))
    def _():
        recv[0] = jnp.zeros(recv.shape[1:], recv.dtype)
        buses[0] = jnp.zeros(buses.shape[1:], buses.dtype)
        adm_side[0] = jnp.zeros(adm_side.shape[1:], adm_side.dtype)
        off_side[0] = jnp.zeros(off_side.shape[1:], off_side.dtype)

    @pl.when(jnp.logical_not(has_right))
    def _():
        recv[nh + 1] = jnp.zeros(recv.shape[1:], recv.dtype)
        buses[nh + 1] = jnp.zeros(buses.shape[1:], buses.dtype)
        adm_side[1] = jnp.zeros(adm_side.shape[1:], adm_side.dtype)
        off_side[1] = jnp.zeros(off_side.shape[1:], off_side.dtype)

    lane = lax.broadcasted_iota(jnp.int32, (1, LANES), 1)
    is_right = lane < LANES // 2

    def adm_row(p, k, h, t, beyond):
        def row_of(t):
            if t < 0:
                return adm_side[0, p, k, h : h + 1, :]
            if t >= tiles:
                return adm_side[1, p, k, h : h + 1, :]
            return adm_ref[p, k, h : h + 1, LANES * t : LANES * (t + 1)]

        return jnp.where(is_right, row_of(t + 1), row_of(t - 1)) if beyond else row_of(t)

    def off_row(k, t, beyond):
        def row_of(t):
            if t < 0:
                return off_side[0, k : k + 1, :]
            if t >= tiles:
                return off_side[1, k : k + 1, :]
            return off_ref[k : k + 1, LANES * t : LANES * (t + 1)]

        return jnp.where(is_right, row_of(t + 1), row_of(t - 1)) if beyond else row_of(t)

    def fill(t, beyond, low, high):
        band = lax.broadcasted_iota(jnp.int32, (high - low, LANES), 0) + low
        shift = LANES if beyond else 0
        masks = [
            band == jnp.bitwise_and(lane + shift + off_row(k, t, beyond), 2 * LANES - 1) for k in range(links)
        ]
        at = 2 * shift
        for h in range(hl):
            d_real, d_imag = adm_row(0, 0, h, t, beyond), adm_row(1, 0, h, t, beyond)
            total_real = jnp.zeros(band.shape, jnp.float32)
            total_imag = jnp.zeros(band.shape, jnp.float32)
            for k in range(links):
                l_real, l_imag = adm_row(0, 1 + k, h, t, beyond), adm_row(1, 1 + k, h, t, beyond)
                total_real += jnp.where(masks[k], d_real * l_real - d_imag * l_imag, 0.0)
                total_imag += jnp.where(masks[k], d_real * l_imag + d_imag * l_real, 0.0)
            weights[h, t, low:high, at : at + LANES] = total_real.astype(jnp.bfloat16)
            weights[h, t, low:high, at + LANES : at + 2 * LANES] = total_imag.astype(jnp.bfloat16)

    for t in range(tiles):
        fill(t, False, 0, LANES + 16)
        fill(t, False, 2 * LANES - 16, 2 * LANES)
        for h in range(hl):
            weights[h, t, LANES + 16 : 2 * LANES - 16, :] = jnp.zeros((LANES - 32, 4 * LANES), jnp.bfloat16)
            weights[h, t, 16 : LANES - 16, 2 * LANES :] = jnp.zeros((LANES - 32, 2 * LANES), jnp.bfloat16)

    pl.semaphore_wait(barrier, nh - 1 + nh * has_left.astype(jnp.int32) + nh * has_right.astype(jnp.int32))

    def remote(src, dst, send_sem, recv_sem, d, by):
        return pltpu.make_async_remote_copy(
            src_ref=src, dst_ref=dst, send_sem=send_sem, recv_sem=recv_sem, device_id={"harm": d, "bus": by}
        )

    def bus_copy(d, slot, by, sems):
        return remote(my_bus, buses.at[slot], sems.at[d], bus_recv.at[slot], d, by)

    def spec_copy(d, slot, by, sems):
        return remote(send.at[d], recv.at[slot], sems.at[d], spec_recv.at[slot], d, by)

    def ret_copy(d, source):
        place = next_ref.at[:, pl.ds(source * hl, hl)]
        return remote(send_back.at[d], place, ret_send.at[d], ret_recv.at[source], d, y)

    def side_copies(side):
        by = y + 1 if side == 0 else y - 1
        start = block - LANES if side == 0 else 0
        return (
            remote(
                adm_ref.at[:, :, :, pl.ds(start, LANES)],
                adm_side.at[side],
                side_send.at[side],
                side_recv.at[side],
                me,
                by,
            ),
            remote(
                off_ref.at[:, pl.ds(start, LANES)],
                off_side.at[side],
                side_send.at[2 + side],
                side_recv.at[2 + side],
                me,
                by,
            ),
        )

    send_right = jnp.logical_and(has_right, me == nh - 1)
    send_left = jnp.logical_and(has_left, me == 0)

    def each(low, body):
        def step(i, carry):
            body(i)
            return carry

        lax.fori_loop(low, nh, step, 0)

    def peer(s):
        return lax.rem(me + s, nh)

    each(1, lambda s: bus_copy(peer(s), me + 1, y, bus_send).start())

    @pl.when(send_right)
    def _():
        each(0, lambda d: bus_copy(d, 0, y + 1, bus_right).start())

    @pl.when(send_left)
    def _():
        each(0, lambda d: bus_copy(d, nh + 1, y - 1, bus_left).start())

    @pl.when(has_right)
    def _():
        for copy in side_copies(0):
            copy.start()

    @pl.when(has_left)
    def _():
        for copy in side_copies(1):
            copy.start()

    each(1, lambda s: spec_copy(peer(s), me + 1, y, spec_send).start())

    @pl.when(send_right)
    def _():
        each(0, lambda d: spec_copy(d, 0, y + 1, left_send).start())

    @pl.when(send_left)
    def _():
        each(0, lambda d: spec_copy(d, nh + 1, y - 1, right_send).start())

    recv[me + 1] = send[me]
    buses[me + 1] = my_bus[...]

    @pl.when(has_left)
    def _():
        for copy in side_copies(0):
            copy.wait_recv()

    @pl.when(has_right)
    def _():
        for copy in side_copies(1):
            copy.wait_recv()

    for t in range(tiles):
        for low, high in ((LANES - 16, LANES + 16), (2 * LANES - 16, 2 * LANES), (0, 16)):
            fill(t, True, low, high)

    each(1, lambda s: bus_copy(peer(s), peer(s) + 1, y, bus_send).wait_recv())

    @pl.when(has_left)
    def _():
        bus_copy(0, 0, y, bus_send).wait_recv()

    @pl.when(has_right)
    def _():
        bus_copy(0, nh + 1, y, bus_send).wait_recv()

    row = lax.broadcasted_iota(jnp.int32, (rows, LANES), 0)
    is_real = row % 8 < conv
    base = jnp.bitwise_and((row // 8 - 1) * sub, 2 * LANES - 1)
    own = 8 * around
    for t in range(tiles):
        near = buses[around * t : around * (t + 1) + 2].astype(jnp.float32).reshape(rows, LANES)
        at_bus = base + near.astype(jnp.int32)
        hits = [at_bus == lane, at_bus == lane + LANES]
        picked = jnp.where(hits[0], 1.0, 0.0)
        pick_real = jnp.where(is_real, picked, 0.0)[8 : 8 + own].astype(jnp.bfloat16)
        pick_imag = jnp.where(is_real, 0.0, picked)[8 : 8 + own].astype(jnp.bfloat16)
        for h in range(hl):
            start_real, start_imag = [], []
            for side in (False, True):
                d_real, d_imag = adm_row(0, 0, h, t, side), adm_row(1, 0, h, t, side)
                start_real.append(jnp.where(hits[side], jnp.where(is_real, d_real, -d_imag), 0.0))
                start_imag.append(jnp.where(hits[side], jnp.where(is_real, d_imag, d_real), 0.0))
            now_real, now_imag = start_real, start_imag
            for last in (False, True):
                state = jnp.concatenate(
                    [jnp.concatenate(now_real, axis=1), jnp.concatenate(now_imag, axis=1)], axis=0
                ).astype(jnp.bfloat16)
                width = 2 * LANES if last else 4 * LANES
                both = jnp.dot(state, weights[h, t, :, 0:width], preferred_element_type=jnp.float32)
                new_real, new_imag = [], []
                for a in range(1 if last else 2):
                    at = 2 * LANES * a
                    left, right = both[:, at : at + LANES], both[:, at + LANES : at + 2 * LANES]
                    new_real.append(start_real[a] + left[:rows] - right[rows:])
                    new_imag.append(start_imag[a] + right[:rows] + left[rows:])
                now_real, now_imag = new_real, new_imag
            real_t = now_real[0].T.astype(jnp.bfloat16)
            imag_t = now_imag[0].T.astype(jnp.bfloat16)
            resp[h, t, own : own + LANES, :] = real_t
            resp[h, t, own + LANES :, :] = imag_t
            chosen = jnp.dot(pick_real, real_t, preferred_element_type=jnp.float32)
            chosen += jnp.dot(pick_imag, imag_t, preferred_element_type=jnp.float32)
            resp[h, t, 0:own, :] = chosen.astype(jnp.bfloat16)

    each(1, lambda s: spec_copy(peer(s), peer(s) + 1, y, spec_send).wait_recv())

    @pl.when(has_left)
    def _():
        spec_copy(0, 0, y, spec_send).wait_recv()

    @pl.when(has_right)
    def _():
        spec_copy(0, nh + 1, y, spec_send).wait_recv()

    arrived = []
    for t in range(tiles):
        for h in range(hl):
            here = recv[around * t : around * (t + 1) + 2, h].astype(jnp.float32)
            arrived.append(here.reshape(rows, LANES).astype(jnp.bfloat16))
            at_conv = jnp.dot(resp[h, t, 0:own, :], arrived[-1], preferred_element_type=jnp.float32)
            at_conv = at_conv.reshape(around, 2, conv, LANES).astype(jnp.bfloat16)
            send_back[around * t : around * (t + 1), :, h] = at_conv
    each(1, lambda s: ret_copy(peer(s), me).start())
    keep = pltpu.make_async_copy(send_back.at[me], next_ref.at[:, pl.ds(me * hl, hl)], local_sem)
    keep.start()
    for t in range(tiles):
        for h in range(hl):
            solved = jnp.dot(resp[h, t, own:, :], arrived[t * hl + h], preferred_element_type=jnp.float32)
            out_ref[:, h, LANES * t : LANES * (t + 1)] = solved.astype(jnp.bfloat16).reshape(2, LANES, LANES)

    each(1, lambda s: bus_copy(peer(s), me + 1, y, bus_send).wait_send())
    each(1, lambda s: spec_copy(peer(s), me + 1, y, spec_send).wait_send())

    @pl.when(has_right)
    def _():
        for copy in side_copies(0):
            copy.wait_send()

    @pl.when(has_left)
    def _():
        for copy in side_copies(1):
            copy.wait_send()

    @pl.when(send_right)
    def _():
        each(0, lambda d: bus_copy(d, 0, y + 1, bus_right).wait_send())
        each(0, lambda d: spec_copy(d, 0, y + 1, left_send).wait_send())

    @pl.when(send_left)
    def _():
        each(0, lambda d: bus_copy(d, nh + 1, y - 1, bus_left).wait_send())
        each(0, lambda d: spec_copy(d, nh + 1, y - 1, right_send).wait_send())

    keep.wait()
    each(1, lambda s: ret_copy(peer(s), me).wait_send())
    each(1, lambda s: ret_copy(peer(s), peer(s)).wait_recv())


def store(volt_ref, next_ref, volt_out, next_out, sems):
    copies = [pltpu.make_async_copy(volt_ref.at[p], volt_out.at[p], sems.at[p]) for p in range(2)]
    copies.append(pltpu.make_async_copy(next_ref, next_out, sems.at[2]))
    for copy in copies:
        copy.start()
    for copy in copies:
        copy.wait()


def local(nh, ny, conv_volt, conv_power, conv_type, type_steep, conv_bus, admittance, link_offset):
    _, orders, conv, snaps = conv_volt.shape
    hl = orders // nh
    block = admittance.shape[3]
    tiles = block // LANES
    around = LANES * nh // block
    rows = 8 * (around + 2)
    span = 2 * orders
    basis = make_basis(orders)
    regrouped = basis.reshape(2, orders, NT).transpose(1, 0, 2).reshape(span, NT)
    per = LANES // conv
    perm = np.zeros((LANES, LANES), np.float32)
    for c in range(conv):
        for k in range(per):
            perm[per * c + k, conv * k + c] = 1.0
    vmem = pl.BlockSpec(memory_space=pltpu.VMEM)
    smem = pl.BlockSpec(memory_space=pltpu.SMEM)
    anywhere = pl.BlockSpec(memory_space=pl.ANY)
    bf16 = jnp.bfloat16
    dma = pltpu.SemaphoreType.DMA
    volt_shape, next_shape = (2, hl, block, snaps), (2, orders, conv, snaps)
    solved = pl.pallas_call(
        functools.partial(kernel, nh, ny),
        out_shape=(pltpu.VMEM(volt_shape, bf16), pltpu.VMEM(next_shape, bf16)),
        in_specs=[vmem, vmem, smem, smem, smem, vmem, vmem, vmem, vmem, vmem, vmem],
        out_specs=(vmem, vmem),
        scratch_shapes=[
            pltpu.VMEM((span, conv * LANES), bf16),
            pltpu.VMEM((nh, hl, 8, LANES), bf16),
            pltpu.VMEM((nh + 2, hl, 8, LANES), bf16),
            pltpu.VMEM((8, LANES), bf16),
            pltpu.VMEM((nh + 2, 8, LANES), bf16),
            pltpu.VMEM((2,) + admittance.shape[:3] + (LANES,), jnp.float32),
            pltpu.VMEM((2, link_offset.shape[0], LANES), jnp.int32),
            pltpu.VMEM((hl, tiles, 2 * LANES, 4 * LANES), bf16),
            pltpu.VMEM((hl, tiles, 8 * around + 2 * LANES, rows), bf16),
            pltpu.VMEM((nh, 2, hl, conv, LANES), bf16),
            dma((nh,)),
            dma((nh + 2,)),
            dma((nh,)),
            dma((nh,)),
            dma((nh,)),
            dma((nh + 2,)),
            dma((nh,)),
            dma((nh,)),
            dma((4,)),
            dma((4,)),
            dma((nh,)),
            dma((nh,)),
            dma,
        ],
        compiler_params=pltpu.CompilerParams(collective_id=0, has_side_effects=True, vmem_limit_bytes=56 * 2**20),
        name="power_flow",
    )(
        conv_volt.reshape(span * conv, snaps),
        conv_power,
        conv_type,
        type_steep,
        conv_bus,
        admittance,
        link_offset,
        jnp.asarray(basis.T, bf16),
        jnp.asarray(regrouped, bf16),
        jnp.asarray(perm, bf16),
        jnp.asarray(perm.T, bf16),
    )
    return pl.pallas_call(
        store,
        out_shape=(jax.ShapeDtypeStruct(volt_shape, bf16), jax.ShapeDtypeStruct(next_shape, bf16)),
        in_specs=[vmem, vmem],
        out_specs=(anywhere, anywhere),
        scratch_shapes=[dma((3,))],
        compiler_params=pltpu.CompilerParams(vmem_limit_bytes=32 * 2**20),
        name="store_results",
    )(*solved)


def solution(mesh):
    in_specs = (
        P(None, None, ("bus", "harm"), None),
        P(("bus", "harm"), None),
        P(("bus", "harm")),
        P(),
        P(("bus", "harm")),
        P(None, None, "harm", "bus"),
        P(None, "bus"),
    )
    out_specs = (P(None, "harm", "bus", None), P(None, None, ("bus", "harm"), None))
    body = functools.partial(local, mesh.shape["harm"], mesh.shape["bus"])
    return jax.shard_map(body, mesh=mesh, in_specs=in_specs, out_specs=out_specs, check_vma=False)
```

```python
import functools
import math

import jax
import jax.numpy as jnp
import numpy as np
from jax import lax
from jax.experimental import pallas as pl
from jax.experimental.pallas import tpu as pltpu
from jax.sharding import PartitionSpec as P

NT = 1024
LANES = 128
CHUNKS = 4


def make_basis(orders):
    samples = np.arange(NT)
    phases = (np.arange(1, orders + 1)[:, None] * samples[None, :] % NT) * (2.0 * math.pi / NT)
    return np.concatenate([np.cos(phases), -np.sin(phases)], axis=0).astype(np.float32)


def kernel(
    nh,
    ny,
    volt_ref,
    power_ref,
    type_ref,
    steep_ref,
    bus_ref,
    adm_ref,
    off_ref,
    fwd_ref,
    inv_ref,
    perm_ref,
    back_ref,
    out_ref,
    next_ref,
    volts,
    send,
    recv,
    my_bus,
    buses,
    adm_side,
    off_side,
    weights,
    resp,
    send_back,
    spec_send,
    spec_recv,
    left_send,
    right_send,
    bus_send,
    bus_recv,
    bus_left,
    bus_right,
    side_send,
    side_recv,
    ret_send,
    ret_recv,
    local_sem,
):
    me = lax.axis_index("harm")
    y = lax.axis_index("bus")
    hl = adm_ref.shape[2]
    block = adm_ref.shape[3]
    links = off_ref.shape[0]
    conv = power_ref.shape[0]
    sub = block // nh
    tiles = block // LANES
    around = LANES // sub
    rows = 8 * (around + 2)
    has_left = y > 0
    has_right = y < ny - 1

    barrier = pltpu.get_barrier_semaphore()

    def greet(d, by):
        pl.semaphore_signal(barrier, inc=1, device_id={"harm": d, "bus": by})

    def greet_peer(s, carry):
        greet(lax.rem(me + s, nh), y)
        return carry

    lax.fori_loop(1, nh, greet_peer, 0)

    @pl.when(has_left)
    def _():
        lax.fori_loop(0, nh, lambda d, c: (greet(d, y - 1), c)[1], 0)

    @pl.when(has_right)
    def _():
        lax.fori_loop(0, nh, lambda d, c: (greet(d, y + 1), c)[1], 0)

    first = (y * nh + me) * sub
    row8 = lax.broadcasted_iota(jnp.int32, (8, LANES), 0) % conv
    numbers = jnp.zeros((8, LANES), jnp.float32)
    for c in range(conv):
        numbers = jnp.where(row8 == c, (bus_ref[c] - first).astype(jnp.float32), numbers)
    my_bus[...] = numbers.astype(jnp.bfloat16)

    @pl.when(jnp.logical_not(has_left))
    def _():
        recv[0] = jnp.zeros(recv.shape[1:], recv.dtype)
        buses[0] = jnp.zeros(buses.shape[1:], buses.dtype)
        adm_side[0] = jnp.zeros(adm_side.shape[1:], adm_side.dtype)
        off_side[0] = jnp.zeros(off_side.shape[1:], off_side.dtype)

    @pl.when(jnp.logical_not(has_right))
    def _():
        recv[nh + 1] = jnp.zeros(recv.shape[1:], recv.dtype)
        buses[nh + 1] = jnp.zeros(buses.shape[1:], buses.dtype)
        adm_side[1] = jnp.zeros(adm_side.shape[1:], adm_side.dtype)
        off_side[1] = jnp.zeros(off_side.shape[1:], off_side.dtype)

    lane = lax.broadcasted_iota(jnp.int32, (1, LANES), 1)
    is_right = lane < LANES // 2

    def adm_row(p, k, h, t, beyond):
        def row_of(t):
            if t < 0:
                return adm_side[0, p, k, h : h + 1, :]
            if t >= tiles:
                return adm_side[1, p, k, h : h + 1, :]
            return adm_ref[p, k, h : h + 1, LANES * t : LANES * (t + 1)]

        return jnp.where(is_right, row_of(t + 1), row_of(t - 1)) if beyond else row_of(t)

    def off_row(k, t, beyond):
        def row_of(t):
            if t < 0:
                return off_side[0, k : k + 1, :]
            if t >= tiles:
                return off_side[1, k : k + 1, :]
            return off_ref[k : k + 1, LANES * t : LANES * (t + 1)]

        return jnp.where(is_right, row_of(t + 1), row_of(t - 1)) if beyond else row_of(t)

    def fill(t, beyond, low, high):
        band = lax.broadcasted_iota(jnp.int32, (high - low, LANES), 0) + low
        shift = LANES if beyond else 0
        masks = [
            band == jnp.bitwise_and(lane + shift + off_row(k, t, beyond), 2 * LANES - 1) for k in range(links)
        ]
        at = 2 * shift
        for h in range(hl):
            d_real, d_imag = adm_row(0, 0, h, t, beyond), adm_row(1, 0, h, t, beyond)
            total_real = jnp.zeros(band.shape, jnp.float32)
            total_imag = jnp.zeros(band.shape, jnp.float32)
            for k in range(links):
                l_real, l_imag = adm_row(0, 1 + k, h, t, beyond), adm_row(1, 1 + k, h, t, beyond)
                total_real += jnp.where(masks[k], d_real * l_real - d_imag * l_imag, 0.0)
                total_imag += jnp.where(masks[k], d_real * l_imag + d_imag * l_real, 0.0)
            weights[h, t, low:high, at : at + LANES] = total_real.astype(jnp.bfloat16)
            weights[h, t, low:high, at + LANES : at + 2 * LANES] = total_imag.astype(jnp.bfloat16)

    for t in range(tiles):
        fill(t, False, 0, LANES + 16)
        fill(t, False, 2 * LANES - 16, 2 * LANES)
        for h in range(hl):
            weights[h, t, LANES + 16 : 2 * LANES - 16, :] = jnp.zeros((LANES - 32, 4 * LANES), jnp.bfloat16)
            weights[h, t, 16 : LANES - 16, 2 * LANES :] = jnp.zeros((LANES - 32, 2 * LANES), jnp.bfloat16)

    pl.semaphore_wait(barrier, nh - 1 + nh * has_left.astype(jnp.int32) + nh * has_right.astype(jnp.int32))

    def remote(src, dst, send_sem, recv_sem, d, by):
        return pltpu.make_async_remote_copy(
            src_ref=src, dst_ref=dst, send_sem=send_sem, recv_sem=recv_sem, device_id={"harm": d, "bus": by}
        )

    def bus_copy(d, slot, by, sems):
        return remote(my_bus, buses.at[slot], sems.at[d], bus_recv.at[slot], d, by)

    def spec_copy(d, slot, by, sems):
        return remote(send.at[d], recv.at[slot], sems.at[d], spec_recv.at[slot], d, by)

    def ret_copy(d, source):
        place = next_ref.at[:, pl.ds(source * hl, hl)]
        return remote(send_back.at[d], place, ret_send.at[d], ret_recv.at[source], d, y)

    def side_copies(side):
        by = y + 1 if side == 0 else y - 1
        start = block - LANES if side == 0 else 0
        return (
            remote(
                adm_ref.at[:, :, :, pl.ds(start, LANES)],
                adm_side.at[side],
                side_send.at[side],
                side_recv.at[side],
                me,
                by,
            ),
            remote(
                off_ref.at[:, pl.ds(start, LANES)],
                off_side.at[side],
                side_send.at[2 + side],
                side_recv.at[2 + side],
                me,
                by,
            ),
        )

    send_right = jnp.logical_and(has_right, me == nh - 1)
    send_left = jnp.logical_and(has_left, me == 0)

    def each(low, body):
        def step(i, carry):
            body(i)
            return carry

        lax.fori_loop(low, nh, step, 0)

    def peer(s):
        return lax.rem(me + s, nh)

    each(1, lambda s: bus_copy(peer(s), me + 1, y, bus_send).start())

    @pl.when(send_right)
    def _():
        each(0, lambda d: bus_copy(d, 0, y + 1, bus_right).start())

    @pl.when(send_left)
    def _():
        each(0, lambda d: bus_copy(d, nh + 1, y - 1, bus_left).start())

    @pl.when(has_right)
    def _():
        for copy in side_copies(0):
            copy.start()

    @pl.when(has_left)
    def _():
        for copy in side_copies(1):
            copy.start()

    span = volt_ref.shape[0] // conv
    per = LANES // conv
    for b in range(span // per):
        block_rows = jnp.dot(
            perm_ref[...], volt_ref[LANES * b : LANES * (b + 1), :], preferred_element_type=jnp.float32
        ).astype(jnp.bfloat16)
        for c in range(conv):
            volts[per * b : per * (b + 1), LANES * c : LANES * (c + 1)] = block_rows[per * c : per * (c + 1), :]
    steep = jnp.concatenate(
        [jnp.full((1, LANES), steep_ref[type_ref[c]], jnp.float32) for c in range(conv)], axis=1
    )
    power = jnp.concatenate([power_ref[c : c + 1, :] for c in range(conv)], axis=1) * NT ** (-0.5)
    part = NT // CHUNKS
    spectra = jnp.zeros((span, conv * LANES), jnp.float32)
    for q in range(CHUNKS):
        wave = jnp.dot(fwd_ref[part * q : part * (q + 1), :], volts[...], preferred_element_type=jnp.float32)
        now = jnp.tanh(steep * wave).astype(jnp.bfloat16)
        spectra = spectra + jnp.dot(
            inv_ref[:, part * q : part * (q + 1)], now, preferred_element_type=jnp.float32
        )
    spectra = (spectra * power).astype(jnp.bfloat16)
    per_dev = 8 * hl
    for b in range(span // per):
        stacked = jnp.concatenate(
            [spectra[per * b : per * (b + 1), LANES * c : LANES * (c + 1)] for c in range(conv)], axis=0
        )
        mixed = jnp.dot(back_ref[...], stacked, preferred_element_type=jnp.float32)
        count = LANES // per_dev
        send[count * b : count * (b + 1)] = mixed.reshape(count, hl, 8, LANES).astype(jnp.bfloat16)

    each(1, lambda s: spec_copy(peer(s), me + 1, y, spec_send).start())

    @pl.when(send_right)
    def _():
        each(0, lambda d: spec_copy(d, 0, y + 1, left_send).start())

    @pl.when(send_left)
    def _():
        each(0, lambda d: spec_copy(d, nh + 1, y - 1, right_send).start())

    recv[me + 1] = send[me]
    buses[me + 1] = my_bus[...]

    @pl.when(has_left)
    def _():
        for copy in side_copies(0):
            copy.wait_recv()

    @pl.when(has_right)
    def _():
        for copy in side_copies(1):
            copy.wait_recv()

    for t in range(tiles):
        for low, high in ((LANES - 16, LANES + 16), (2 * LANES - 16, 2 * LANES), (0, 16)):
            fill(t, True, low, high)

    each(1, lambda s: bus_copy(peer(s), peer(s) + 1, y, bus_send).wait_recv())

    @pl.when(has_left)
    def _():
        bus_copy(0, 0, y, bus_send).wait_recv()

    @pl.when(has_right)
    def _():
        bus_copy(0, nh + 1, y, bus_send).wait_recv()

    row = lax.broadcasted_iota(jnp.int32, (rows, LANES), 0)
    is_real = row % 8 < conv
    base = jnp.bitwise_and((row // 8 - 1) * sub, 2 * LANES - 1)
    own = 8 * around
    for t in range(tiles):
        near = buses[around * t : around * (t + 1) + 2].astype(jnp.float32).reshape(rows, LANES)
        at_bus = base + near.astype(jnp.int32)
        hits = [at_bus == lane, at_bus == lane + LANES]
        picked = jnp.where(hits[0], 1.0, 0.0)
        pick_real = jnp.where(is_real, picked, 0.0)[8 : 8 + own].astype(jnp.bfloat16)
        pick_imag = jnp.where(is_real, 0.0, picked)[8 : 8 + own].astype(jnp.bfloat16)
        for h in range(hl):
            start_real, start_imag = [], []
            for side in (False, True):
                d_real, d_imag = adm_row(0, 0, h, t, side), adm_row(1, 0, h, t, side)
                start_real.append(jnp.where(hits[side], jnp.where(is_real, d_real, -d_imag), 0.0))
                start_imag.append(jnp.where(hits[side], jnp.where(is_real, d_imag, d_real), 0.0))
            now_real, now_imag = start_real, start_imag
            for last in (False, True):
                state = jnp.concatenate(
                    [jnp.concatenate(now_real, axis=1), jnp.concatenate(now_imag, axis=1)], axis=0
                ).astype(jnp.bfloat16)
                width = 2 * LANES if last else 4 * LANES
                both = jnp.dot(state, weights[h, t, :, 0:width], preferred_element_type=jnp.float32)
                new_real, new_imag = [], []
                for a in range(1 if last else 2):
                    at = 2 * LANES * a
                    left, right = both[:, at : at + LANES], both[:, at + LANES : at + 2 * LANES]
                    new_real.append(start_real[a] + left[:rows] - right[rows:])
                    new_imag.append(start_imag[a] + right[:rows] + left[rows:])
                now_real, now_imag = new_real, new_imag
            real_t = now_real[0].T.astype(jnp.bfloat16)
            imag_t = now_imag[0].T.astype(jnp.bfloat16)
            resp[h, t, own : own + LANES, :] = real_t
            resp[h, t, own + LANES :, :] = imag_t
            chosen = jnp.dot(pick_real, real_t, preferred_element_type=jnp.float32)
            chosen += jnp.dot(pick_imag, imag_t, preferred_element_type=jnp.float32)
            resp[h, t, 0:own, :] = chosen.astype(jnp.bfloat16)

    each(1, lambda s: spec_copy(peer(s), peer(s) + 1, y, spec_send).wait_recv())

    @pl.when(has_left)
    def _():
        spec_copy(0, 0, y, spec_send).wait_recv()

    @pl.when(has_right)
    def _():
        spec_copy(0, nh + 1, y, spec_send).wait_recv()

    arrived = []
    for t in range(tiles):
        for h in range(hl):
            here = recv[around * t : around * (t + 1) + 2, h].astype(jnp.float32)
            arrived.append(here.reshape(rows, LANES).astype(jnp.bfloat16))
            at_conv = jnp.dot(resp[h, t, 0:own, :], arrived[-1], preferred_element_type=jnp.float32)
            at_conv = at_conv.reshape(around, 2, conv, LANES).astype(jnp.bfloat16)
            send_back[around * t : around * (t + 1), :, h] = at_conv
    each(1, lambda s: ret_copy(peer(s), me).start())
    keep = pltpu.make_async_copy(send_back.at[me], next_ref.at[:, pl.ds(me * hl, hl)], local_sem)
    keep.start()
    for t in range(tiles):
        for h in range(hl):
            solved = jnp.dot(resp[h, t, own:, :], arrived[t * hl + h], preferred_element_type=jnp.float32)
            out_ref[:, h, LANES * t : LANES * (t + 1)] = solved.astype(jnp.bfloat16).reshape(2, LANES, LANES)

    each(1, lambda s: bus_copy(peer(s), me + 1, y, bus_send).wait_send())
    each(1, lambda s: spec_copy(peer(s), me + 1, y, spec_send).wait_send())

    @pl.when(has_right)
    def _():
        for copy in side_copies(0):
            copy.wait_send()

    @pl.when(has_left)
    def _():
        for copy in side_copies(1):
            copy.wait_send()

    @pl.when(send_right)
    def _():
        each(0, lambda d: bus_copy(d, 0, y + 1, bus_right).wait_send())
        each(0, lambda d: spec_copy(d, 0, y + 1, left_send).wait_send())

    @pl.when(send_left)
    def _():
        each(0, lambda d: bus_copy(d, nh + 1, y - 1, bus_left).wait_send())
        each(0, lambda d: spec_copy(d, nh + 1, y - 1, right_send).wait_send())

    keep.wait()
    each(1, lambda s: ret_copy(peer(s), me).wait_send())
    each(1, lambda s: ret_copy(peer(s), peer(s)).wait_recv())


def store(volt_ref, next_ref, volt_out, next_out, sems):
    copies = [pltpu.make_async_copy(volt_ref.at[p], volt_out.at[p], sems.at[p]) for p in range(2)]
    copies.append(pltpu.make_async_copy(next_ref, next_out, sems.at[2]))
    for copy in copies:
        copy.start()
    for copy in copies:
        copy.wait()


def local(nh, ny, conv_volt, conv_power, conv_type, type_steep, conv_bus, admittance, link_offset):
    _, orders, conv, snaps = conv_volt.shape
    hl = orders // nh
    block = admittance.shape[3]
    tiles = block // LANES
    around = LANES * nh // block
    rows = 8 * (around + 2)
    span = 2 * orders
    basis = make_basis(orders)
    regrouped = basis.reshape(2, orders, NT).transpose(1, 0, 2).reshape(span, NT)
    per = LANES // conv
    perm = np.zeros((LANES, LANES), np.float32)
    for c in range(conv):
        for k in range(per):
            perm[per * c + k, conv * k + c] = 1.0
    vmem = pl.BlockSpec(memory_space=pltpu.VMEM)
    smem = pl.BlockSpec(memory_space=pltpu.SMEM)
    anywhere = pl.BlockSpec(memory_space=pl.ANY)
    bf16 = jnp.bfloat16
    dma = pltpu.SemaphoreType.DMA
    volt_shape, next_shape = (2, hl, block, snaps), (2, orders, conv, snaps)
    solved = pl.pallas_call(
        functools.partial(kernel, nh, ny),
        out_shape=(pltpu.VMEM(volt_shape, bf16), pltpu.VMEM(next_shape, bf16)),
        in_specs=[vmem, vmem, smem, smem, smem, vmem, vmem, vmem, vmem, vmem, vmem],
        out_specs=(vmem, vmem),
        scratch_shapes=[
            pltpu.VMEM((span, conv * LANES), bf16),
            pltpu.VMEM((nh, hl, 8, LANES), bf16),
            pltpu.VMEM((nh + 2, hl, 8, LANES), bf16),
            pltpu.VMEM((8, LANES), bf16),
            pltpu.VMEM((nh + 2, 8, LANES), bf16),
            pltpu.VMEM((2,) + admittance.shape[:3] + (LANES,), jnp.float32),
            pltpu.VMEM((2, link_offset.shape[0], LANES), jnp.int32),
            pltpu.VMEM((hl, tiles, 2 * LANES, 4 * LANES), bf16),
            pltpu.VMEM((hl, tiles, 8 * around + 2 * LANES, rows), bf16),
            pltpu.VMEM((nh, 2, hl, conv, LANES), bf16),
            dma((nh,)),
            dma((nh + 2,)),
            dma((nh,)),
            dma((nh,)),
            dma((nh,)),
            dma((nh + 2,)),
            dma((nh,)),
            dma((nh,)),
            dma((4,)),
            dma((4,)),
            dma((nh,)),
            dma((nh,)),
            dma,
        ],
        compiler_params=pltpu.CompilerParams(collective_id=0, has_side_effects=True, vmem_limit_bytes=56 * 2**20),
        name="power_flow",
    )(
        conv_volt.reshape(span * conv, snaps),
        conv_power,
        conv_type,
        type_steep,
        conv_bus,
        admittance,
        link_offset,
        jnp.asarray(basis.T, bf16),
        jnp.asarray(regrouped, bf16),
        jnp.asarray(perm, bf16),
        jnp.asarray(perm.T, bf16),
    )
    return pl.pallas_call(
        store,
        out_shape=(jax.ShapeDtypeStruct(volt_shape, bf16), jax.ShapeDtypeStruct(next_shape, bf16)),
        in_specs=[vmem, vmem],
        out_specs=(anywhere, anywhere),
        scratch_shapes=[dma((3,))],
        compiler_params=pltpu.CompilerParams(vmem_limit_bytes=32 * 2**20),
        name="store_results",
    )(*solved)


def solution(mesh):
    in_specs = (
        P(None, None, ("bus", "harm"), None),
        P(("bus", "harm"), None),
        P(("bus", "harm")),
        P(),
        P(("bus", "harm")),
        P(None, None, "harm", "bus"),
        P(None, "bus"),
    )
    out_specs = (P(None, "harm", "bus", None), P(None, None, ("bus", "harm"), None))
    body = functools.partial(local, mesh.shape["harm"], mesh.shape["bus"])
    return jax.shard_map(body, mesh=mesh, in_specs=in_specs, out_specs=out_specs, check_vma=False)
```
